32 devices in a mesh: blk: 16 (over z, x, core), narrow: 2 (over y).
Axes of the slice: x: 2, y: 2, z: 4, core: 2. Of those that a mesh axis runs over, the one named last changes fastest.
Arguments:
- rhs: float32 [6144, 256], P('blk', 'narrow'), may hold values from -6 to 6
- zo: float32 [6144, 64], P('blk'), may hold values from -0.109375 to 0.109375
- e_diag: float32 [64, 96, 96], P('blk'), may hold values from -0.18 to 0.18
- a_off: float32 [64, 3, 96, 96], P('blk'), may hold values from -0.18 to 0.18
- e_off: float32 [64, 3, 96, 96], P('blk'), may hold values from -0.09 to 0.09
- col_index: int32 [64, 3], P('blk'), may hold values from 0 to 63, as said below
- inv_diag: float32 [2, 64, 96, 96], P(None, 'blk'), may hold values from -0.625 to 0.625
- shifts: float32 [2], replicated, may hold values from 0.5 to 2
Outputs:
- residual: float32 [6144, 256], P('blk', 'narrow')
- cross: float32 [64, 2, 256], P(('blk', 'narrow'))
The draws below stay inside these ranges and needn't reach their ends.
Inputs may be any that keep to these rules, and one draw needn't show every extreme that they name: `col_index`: each block column index differs from its own block row by 1 or 2 in either direction, near the ends of the range reflected to the other side; the three indices of a row may repeat.
All inputs are finite; a program needn't handle non-finite values.
Results may differ from the reference program's by a relative error of at most 0.0001.
Values sent between devices are 32-bit elements; how exact they have to be, the bound alone decides.
A program may use at most 64 MiB of HBM per device.

```python
import math
import jax
import jax.numpy as jnp
from jax import lax

BD = 96
CPL = 3
SWEEPS = 8
NB = 64
NN = 6144
K = 256
KO = 64


def draw_col_index(key, part):
    block_rows = jnp.arange(NB, dtype=jnp.int32)
    dropped = jax.random.randint(key, (NB,), 0, 4).astype(jnp.int32)
    dropped = jnp.where(block_rows == NB - 2, 0, dropped)
    dropped = jnp.where(block_rows == 1, 3, dropped)
    offsets = jnp.array([-2, -1, 1, 2], jnp.int32)
    slots = jnp.arange(3, dtype=jnp.int32)[None, :]
    picks = slots + (slots >= dropped[:, None]).astype(jnp.int32)
    chosen = offsets[picks]
    columns = block_rows[:, None] + chosen
    outside = (columns < 0) | (columns >= NB)
    return jnp.where(outside, block_rows[:, None] - chosen, columns).astype(jnp.int32)


def strengthened(result, stream_key, source, target, parts, factor):
    owner, partner = [(jnp.arange(result.shape[position]) // (result.shape[position] // parts)).reshape([-1 if axis == position else 1 for axis in range(result.ndim)]) for position in (source, target)]
    chosen = jax.random.permutation(stream_key, parts)[partner]
    strong = (owner == chosen) | (owner == (partner + parts // 2) % parts)
    return jnp.where(strong, factor * result, result)


def shard_levels(own_key, shape, cuts, least, largest):
    gain, own = 1.0, jax.random.fold_in(own_key, 6)
    for position, shards_of in cuts:
        steps = jnp.exp(jax.random.uniform(jax.random.fold_in(own, position), (shards_of,), jnp.float32, least / len(cuts), largest / len(cuts)))
        gain = gain * jnp.repeat(steps, shape[position] // shards_of).reshape([-1 if axis == position else 1 for axis in range(len(shape))])
    return gain


def centred(stream_key, shape, deviation, most, split=(), held_as=jnp.bfloat16):
    values = deviation * jax.random.normal(stream_key, shape, jnp.float32)
    if split:
        values = values * shard_levels(stream_key, shape, split, -0.22, 0.18)
    return jnp.clip(values, -most, most).astype(held_as)


def bell_draw_with(key, shape, spread, reach, shards, heavy, kind=jnp.bfloat16):
    drawn = spread * jax.random.normal(key, shape, jnp.float32)
    if shards:
        drawn = drawn * shard_levels(key, shape, shards, -0.22, 0.18)
    return jnp.clip(strengthened(drawn, jax.random.fold_in(key, 3), *heavy), -reach, reach).astype(kind)


def setup_inputs(seed: int = 0) -> dict:
    arg_keys = jax.random.split(jax.random.key(seed), 9)
    return {
        "rhs": centred(arg_keys[0], (NN, K), 1.0, 6.0, ((0, 16), (1, 2)), jnp.float32),
        "zo": bell_draw_with(arg_keys[1], (NN, KO), NN ** -0.5, 0.109375, ((0, 16),), (0, 1, 16, 2.0), jnp.float32),
        "e_diag": centred(arg_keys[2], (NB, BD, BD), 0.0306, 0.18, ((0, 16),), jnp.float32),
        "a_off": centred(arg_keys[3], (NB, CPL, BD, BD), 0.0306, 0.18, ((0, 16),), jnp.float32),
        "e_off": centred(arg_keys[4], (NB, CPL, BD, BD), 0.0153, 0.09, ((0, 16),), jnp.float32),
        "col_index": draw_col_index(jax.random.fold_in(arg_keys[8], 71), 0),
        "inv_diag": centred(arg_keys[6], (2, NB, BD, BD), BD ** -0.5, 0.625, ((1, 16),), jnp.float32),
        "shifts": jnp.clip(jnp.exp(jax.random.uniform(arg_keys[7], (2,), jnp.float32, math.log(0.5), math.log(2.0))), 0.5, 2.0),
    }


precise = lax.Precision.HIGHEST

def block_product(matrices, field):
    return jnp.einsum('nab,nbk->nak', matrices, field, precision=precise)

def coupled_product(coupling, col_index, field):
    picked = jnp.take(field, col_index, axis=0)
    return jnp.einsum('nsab,nsbk->nak', coupling, picked, precision=precise)

def reference(rhs, zo, e_diag, a_off, e_off, col_index, inv_diag, shifts):
    columns = rhs.shape[1]
    current = rhs.reshape(NB, BD, columns)
    images = []
    for which in range(2):
        shift_value = shifts[which]
        coupling = a_off - shift_value * e_off
        inverse = inv_diag[which]
        iterate = block_product(inverse, current)
        for sweep in range(SWEEPS):
            iterate = block_product(inverse, current - coupled_product(coupling, col_index, iterate))
        mass_image = block_product(e_diag, iterate) + coupled_product(e_off, col_index, iterate)
        current = current + 2.0 * shift_value * mass_image
        images.append(jnp.sqrt(2.0 * shift_value) * mass_image)
    stacked = jnp.stack(images, axis=2).reshape(NN, 2, columns)
    cross = jnp.einsum('ro,rsk->osk', zo, stacked, precision=precise)
    return (current.reshape(NN, columns), cross)
```

```python
import functools

import jax
import jax.numpy as jnp
from jax import lax
from jax.experimental import pallas as pl
from jax.experimental.pallas import tpu as pltpu
from jax.sharding import PartitionSpec as P

SWEEPS = 8
DEPTH = 3
LEVELS = SWEEPS + 1
CYCLES = LEVELS // DEPTH
OFFSETS = (-2, -1, 1, 2)
LANES = 128
MASS = 2
HOOKS = 6
EDGE, FREE = 0, 1
f32, bf16 = jnp.float32, jnp.bfloat16


def split(x):
    high = x.astype(bf16)
    return high, (x - high.astype(f32)).astype(bf16)


def beside(x):
    return jnp.concatenate(split(x), axis=1)


def below(x):
    return jnp.concatenate(split(x), axis=0)


def product(matrix, field):
    whole = jnp.dot(matrix, field, preferred_element_type=f32)
    rows, cols = whole.shape[0] // 2, whole.shape[1] // 2
    return (whole[:rows, :cols] + whole[:rows, cols:]) + (whole[rows:, :cols] + whole[rows:, cols:])


def kernel(
    count, others, size,
    rhs_hbm, zo_hbm, e_diag_hbm, a_off_hbm, e_off_hbm, col_ref, inv_hbm, shift_ref,
    res_ref, cross_ref,
    far_out, far_in, near_out, near_in, mat_out, mat_in,
    base, image, band, by_x, by_n, by_y, by_m, far_x, far_y, inverse, zot, partial, outbox, inbox,
    far_send, far_recv, near_send, near_recv, mat_send, mat_recv, cross_send, cross_recv, tokens,
    rhs_ref, zo_ref, e_diag_ref, a_off_ref, e_off_ref, inv_ref, load_sem,
):
    me = lax.axis_index("blk")
    mine = lax.axis_index("narrow")
    devices = count * others
    rank = me * others + mine
    parity = lax.rem(me, 2)
    sign = 1 - 2 * parity
    has_far = jnp.logical_and(me != 0, me != count - 1)
    near_id = me + sign
    far_id = jnp.where(has_far, me - sign, near_id)
    per = outbox.shape[2]
    pair = 2 * size
    rounds = (count - 2).bit_length()
    short = rounds <= HOOKS

    def row_of(c):
        return c + parity * (3 - 2 * c)

    def rows_of(c):
        return pl.ds(pl.multiple_of(row_of(c) * size, 8), size)

    loads = [
        pltpu.make_async_copy(source, target, load_sem.at[k])
        for k, (source, target) in enumerate((
            (rhs_hbm, rhs_ref), (inv_hbm, inv_ref), (a_off_hbm, a_off_ref), (e_off_hbm, e_off_ref),
            (e_diag_hbm, e_diag_ref), (zo_hbm, zo_ref),
        ))
    ]
    barrier = pltpu.get_barrier_semaphore()
    for load in loads:
        load.start()

    def greet(**where):
        pl.semaphore_signal(barrier, inc=1, device_id=where, device_id_type=pl.DeviceIdType.MESH)

    def everyone(act):
        def at(k, carry):
            b = lax.rem(k + me + count // 2, count)
            for n in range(others):
                @pl.when(jnp.logical_or(b != me, n != mine))
                def _():
                    act(b, n)
            return carry
        lax.fori_loop(0, count, at, 0)

    if short:
        greet(blk=near_id)

        @pl.when(has_far)
        def _():
            greet(blk=far_id)

        for k in range(1, others):
            greet(narrow=lax.rem(mine + k, others))
        greeted = others + jnp.where(has_far, 1, 0)
    else:
        everyone(lambda b, n: greet(blk=b, narrow=n))
        greeted = devices - 1

    @pl.when(jnp.logical_not(has_far))
    def _():
        def clear(s, carry):
            far_in[s] = jnp.zeros((DEPTH, pair, LANES), f32)
            return carry
        lax.fori_loop(0, 2 * CYCLES, clear, 0)
        mat_in[...] = jnp.zeros_like(mat_in)

    def tell(t):
        if not short or t >= rounds:
            return
        d = 1 << t
        for up, there, target in (
            (0, me + d < count, jnp.minimum(me + d, count - 1)),
            (1, me - d >= 0, jnp.maximum(me - d, 0)),
        ):
            @pl.when(there)
            def _():
                pl.semaphore_signal(
                    tokens.at[t, up], inc=1, device_id={"blk": target}, device_id_type=pl.DeviceIdType.MESH
                )

    def hear(t):
        if not short or t >= rounds:
            return
        d = 1 << t
        for up, there in ((0, me - d >= 0), (1, me + d < count)):
            @pl.when(there)
            def _():
                pl.semaphore_wait(tokens.at[t, up], 1)

        tell(t + 1)

    def far_copy(f, k):
        return pltpu.make_async_remote_copy(
            src_ref=far_out.at[f, k], dst_ref=far_in.at[f, k],
            send_sem=far_send.at[f, k], recv_sem=far_recv.at[f, k],
            device_id={"blk": far_id}, device_id_type=pl.DeviceIdType.MESH,
        )

    def near_copy(s):
        return pltpu.make_async_remote_copy(
            src_ref=near_out.at[s], dst_ref=near_in.at[s],
            send_sem=near_send.at[s], recv_sem=near_recv.at[s],
            device_id={"blk": near_id}, device_id_type=pl.DeviceIdType.MESH,
        )

    def mat_copy(which):
        return pltpu.make_async_remote_copy(
            src_ref=mat_out.at[which], dst_ref=mat_in.at[which],
            send_sem=mat_send.at[which], recv_sem=mat_recv.at[which],
            device_id={"blk": far_id}, device_id_type=pl.DeviceIdType.MESH,
        )

    def if_far(act):
        pl.when(has_far)(act)

    def send_far(f, k, value):
        far_out[f, k] = value
        if_far(lambda: far_copy(f, k).start())

    def send_near(s, value):
        near_out[s] = value
        near_copy(s).start()

    def from_far(f, k):
        if_far(lambda: far_copy(f, k).wait_recv())
        return far_in[f, k]

    def from_near(s):
        near_copy(s).wait_recv()
        return near_in[s]

    filler = jnp.zeros((LANES - size, 2 * LANES), bf16)

    def field(value):
        return jnp.concatenate([beside(value[:size]), filler, beside(value[size:]), filler], axis=0)

    def solved(which, c, value):
        return product(inverse[which, c], beside(value))

    def put(matrix, which, row, k, block):
        rows = matrix.shape[1] // 2
        high, low = split(block)
        lanes = slice(k * LANES, (k + 1) * LANES)
        matrix[which, row * size:(row + 1) * size, lanes] = high
        matrix[which, rows + row * size:rows + (row + 1) * size, lanes] = low

    nothing = jnp.zeros((size, LANES), f32)

    def place(which, row, blocks):
        def at(c):
            return blocks[c - row] if c - row in blocks else nothing

        for k in range(2):
            put(by_x, which, row, k, at(k))
            put(by_n, which, row, k, at(2 + k))
            if row < 2:
                put(by_y, which, row, k, at(-1 - k))
            else:
                put(by_m, which, row - 2, k, at(5 - k))

    def build_band(c):
        row = row_of(c)
        for k, offset in enumerate(OFFSETS):
            total_a = jnp.zeros((size, size), f32)
            total_e = jnp.zeros((size, size), f32)
            for s in range(3):
                weight = jnp.where(col_ref[row, s] == me * 4 + row + sign * offset, f32(1.0), f32(0.0))
                total_a = total_a + weight * a_off_ref[row, s]
                total_e = total_e + weight * e_off_ref[row, s]
            band[0, c, :, k * LANES:k * LANES + size] = total_a
            band[1, c, :, k * LANES:k * LANES + size] = total_e

    def build_sweep(which, rows):
        q = shift_ref[which]
        for c in rows:
            merged = product(inverse[which, c], beside(band[0, c] - q * band[1, c]))
            blocks = {o: merged[:, k * LANES:(k + 1) * LANES] for k, o in enumerate(OFFSETS)}
            if c == 0:
                mat_out[which, 0] = blocks[-1]
                mat_out[which, 1] = blocks[-2]
                mat_out[which, 3] = blocks[1]
            if c == 1:
                mat_out[which, 2] = blocks[-2]
                mat_out[which, 4] = blocks[-1]
                if_far(lambda: mat_copy(which).start())
            place(which, c, blocks)

    def build_far(which):
        if_far(lambda: mat_copy(which).wait_recv())
        put(far_x, which, 0, 0, mat_in[which, 0])
        put(far_x, which, 0, 1, mat_in[which, 1])
        put(far_x, which, 1, 0, mat_in[which, 2])
        put(far_x, which, 1, 1, nothing)
        put(far_y, which, 0, 0, nothing)
        put(far_y, which, 0, 1, mat_in[which, 3])
        put(far_y, which, 1, 0, mat_in[which, 4])
        put(far_y, which, 1, 1, nothing)

    def build_mass():
        for c in range(4):
            blocks = {o: band[1, c, :, k * LANES:(k + 1) * LANES] for k, o in enumerate(OFFSETS)}
            blocks[0] = jnp.concatenate([e_diag_ref[row_of(c)], jnp.zeros((size, LANES - size), f32)], axis=1)
            place(MASS, c, blocks)

    def cycle(which, f, s, last, beside_far=None, late=None):
        x0, n0 = far_out[f, EDGE], near_out[s]
        base_x, base_n = base[0], base[1]
        fx0 = field(x0)
        gn = product(by_n[which], field(n0))
        r0 = base_x - gn[:pair]
        send_far(f, FREE, r0)
        gx = product(by_x[which], fx0)
        p0 = r0 - gx[:pair]
        n1 = ((base_n - gn[pair:]) - gx[pair:]) - product(by_m[which], field(from_near(s)))
        send_near(s + 1, n1)
        gn = product(by_n[which], field(n1))
        r1 = base_x - gn[:pair]
        send_far(f, FREE + 1, r1)
        t2 = (base_n - gn[pair:]) - product(by_m[which], field(from_near(s + 1)))
        if late is None:
            hx = product(far_x[which], fx0)
        if beside_far is not None:
            beside_far()
        fy0 = field(from_far(f, EDGE))
        x1 = p0 - product(by_y[which], fy0)
        fx1 = field(x1)
        gx = product(by_x[which], fx1)
        n2 = t2 - gx[pair:]
        send_near(s + 2, n2)
        if late is not None:
            late()
            hx = product(far_x[which], fx0)
        y1 = (from_far(f, FREE) - product(far_y[which], fy0)) - hx
        fy1 = field(y1)
        x2 = (r1 - gx[:pair]) - product(by_y[which], fy1)
        known = product(far_y[which], fy1) + product(far_x[which], fx1)
        then = MASS if last else which
        gx = product(by_x[then], field(x2))
        gn = product(by_n[then], field(n2))
        gm = product(by_m[then], field(from_near(s + 2)))
        at_n = (gx[pair:] + gn[pair:]) + gm

        def at_x():
            y2 = from_far(f, FREE + 1) - known
            return (gx[:pair] + gn[:pair]) + product(by_y[then], field(y2))

        if last:
            return at_n, at_x
        send_near(s + 3, base_n - at_n)
        send_far(f + 1, EDGE, base_x - at_x())

    def start_with(which, half, values):
        for k, value in enumerate(values):
            base[half, k * size:(k + 1) * size] = solved(which, 2 * half + k, value)

    loads[0].wait()
    loads[1].wait()
    for c in range(4):
        inverse[0, c] = below(inv_ref[0, row_of(c)])
    for half in range(2):
        start_with(0, half, [rhs_ref[rows_of(2 * half + k), :] for k in range(2)])
    pl.semaphore_wait(barrier, greeted)
    send_far(0, EDGE, base[0])
    send_near(0, base[1])
    tell(0)
    band[...] = jnp.zeros_like(band)
    for load in loads[2:]:
        load.wait()
    for half in range(2):
        for c in (2 * half, 2 * half + 1):
            build_band(c)
        build_sweep(0, (2 * half, 2 * half + 1))

    def post(which):
        def act(b, n):
            pltpu.make_async_remote_copy(
                src_ref=outbox.at[which, b * others + n],
                dst_ref=inbox.at[which, rank],
                send_sem=cross_send.at[which],
                recv_sem=cross_recv.at[which],
                device_id={"blk": b, "narrow": n},
                device_id_type=pl.DeviceIdType.MESH,
            ).start()

        everyone(act)

    def first_aside():
        hear(0)
        for c in range(4):
            inverse[1, c] = below(inv_ref[1, row_of(c)])
        build_mass()

    def second_aside():
        hear(1)
        build_sweep(1, range(4))

    def third_aside():
        hear(2)
        build_far(1)
        zot[...] = below(zo_ref[...])

    def last_aside():
        for t in range(4, HOOKS):
            hear(t)
        post(0)

    def step(c, carry):
        cycle(1, CYCLES + c, LEVELS + DEPTH * c, False)
        return carry

    for which in range(2):
        f, s = which * CYCLES, which * LEVELS
        if which == 0:
            cycle(0, f, s, False, first_aside, lambda: build_far(0))
            cycle(0, f + 1, s + DEPTH, False, second_aside)
        else:
            lax.fori_loop(0, CYCLES - 1, step, 0)
        aside = last_aside if which == 1 else third_aside
        at_n, at_x = cycle(which, f + CYCLES - 1, s + DEPTH * (CYCLES - 1), True, aside)

        q = shift_ref[which]
        root = jnp.sqrt(jnp.full((1, LANES), 2.0 * q, f32))
        for half, value in ((1, at_n), (0, at_x())):
            after = []
            for k in range(2):
                mass = value[k * size:(k + 1) * size]
                rows = rows_of(2 * half + k)
                before = rhs_ref[rows, :] if which == 0 else res_ref[rows, :]
                after.append(before + (2.0 * q) * mass)
                res_ref[rows, :] = after[k]
                image[rows, :] = root * mass
            if which == 0:
                start_with(1, half, after)
                if half == 1:
                    send_near(LEVELS, base[1])
                else:
                    send_far(CYCLES, EDGE, base[0])
        if which == 0:
            hear(3)

        partial[...] = product(zot[...], beside(image[...]))

        def pack(d, carry):
            outbox[which, d] = partial[pl.ds(d * per, per), :]
            return carry

        lax.fori_loop(0, devices, pack, 0, unroll=8)

        if which == 1:
            post(1)
        inbox[which, rank] = outbox[which, rank]

    for which in range(2):
        most = pl.ds(0, devices - 1)
        pltpu.make_async_copy(outbox.at[which, most], inbox.at[which, most], cross_recv.at[which]).wait()
        for n in range(others):
            total = inbox[which, n]
            for b in range(1, count):
                total = total + inbox[which, b * others + n]
            cross_ref[:, which, n * LANES:(n + 1) * LANES] = total
        pltpu.make_async_copy(outbox.at[which, most], inbox.at[which, most], cross_send.at[which]).wait()

    @pl.when(has_far)
    def _():
        def settle(f, carry):
            for k in range(DEPTH):
                far_copy(f, k).wait_send()
            return carry
        lax.fori_loop(0, 2 * CYCLES, settle, 0)
        for which in range(2):
            mat_copy(which).wait_send()

    def settle_near(s, carry):
        near_copy(s).wait_send()
        return carry

    lax.fori_loop(0, 2 * LEVELS, settle_near, 0)


def shards(count, others, rhs, zo, e_diag, a_off, e_off, col_index, inv_diag, shifts):
    row_count, col_width = rhs.shape
    size = e_diag.shape[1]
    ko = zo.shape[1]
    devices = count * others
    per = ko // devices
    assert row_count == 4 * size and col_width == LANES and count % 2 == 0
    vmem = pl.BlockSpec(memory_space=pltpu.VMEM)
    smem = pl.BlockSpec(memory_space=pltpu.SMEM)
    hbm = pl.BlockSpec(memory_space=pl.ANY)
    pair = 2 * size
    width = 2 * LANES
    return pl.pallas_call(
        functools.partial(kernel, count, others, size),
        out_shape=(
            jax.ShapeDtypeStruct((row_count, col_width), f32),
            jax.ShapeDtypeStruct((per, 2, others * LANES), f32),
        ),
        in_specs=[hbm, hbm, hbm, hbm, hbm, smem, hbm, smem],
        out_specs=(vmem, vmem),
        scratch_shapes=[
            pltpu.VMEM((2 * CYCLES, DEPTH, pair, LANES), f32),
            pltpu.VMEM((2 * CYCLES, DEPTH, pair, LANES), f32),
            pltpu.VMEM((2 * LEVELS, pair, LANES), f32),
            pltpu.VMEM((2 * LEVELS, pair, LANES), f32),
            pltpu.VMEM((2, 5, size, LANES), f32),
            pltpu.VMEM((2, 5, size, LANES), f32),
            pltpu.VMEM((2, pair, LANES), f32),
            pltpu.VMEM((row_count, LANES), f32),
            pltpu.VMEM((2, 4, size, 4 * LANES), f32),
            pltpu.VMEM((3, 4 * pair, width), bf16),
            pltpu.VMEM((3, 4 * pair, width), bf16),
            pltpu.VMEM((3, 2 * pair, width), bf16),
            pltpu.VMEM((3, 2 * pair, width), bf16),
            pltpu.VMEM((2, 2 * pair, width), bf16),
            pltpu.VMEM((2, 2 * pair, width), bf16),
            pltpu.VMEM((2, 4, 2 * size, size), bf16),
            pltpu.VMEM((2 * ko, row_count), bf16),
            pltpu.VMEM((ko, LANES), f32),
            pltpu.VMEM((2, devices, per, LANES), f32),
            pltpu.VMEM((2, devices, per, LANES), f32),
            pltpu.SemaphoreType.DMA((2 * CYCLES, DEPTH)),
            pltpu.SemaphoreType.DMA((2 * CYCLES, DEPTH)),
            pltpu.SemaphoreType.DMA((2 * LEVELS,)),
            pltpu.SemaphoreType.DMA((2 * LEVELS,)),
            pltpu.SemaphoreType.DMA((2,)),
            pltpu.SemaphoreType.DMA((2,)),
            pltpu.SemaphoreType.DMA((2,)),
            pltpu.SemaphoreType.DMA((2,)),
            pltpu.SemaphoreType.REGULAR((HOOKS, 2)),
            *(pltpu.VMEM(x.shape, f32) for x in (rhs, zo.T, e_diag, a_off, e_off, inv_diag)),
            pltpu.SemaphoreType.DMA((6,)),
        ],
        compiler_params=pltpu.CompilerParams(
            collective_id=0, has_side_effects=True, vmem_limit_bytes=48 * 1024 * 1024
        ),
    )(rhs, zo.T, e_diag, a_off, e_off, col_index, inv_diag, shifts)


def solution(mesh):
    placed = (
        P("blk", "narrow"),
        P("blk", None),
        P("blk", None, None),
        P("blk", None, None, None),
        P("blk", None, None, None),
        P("blk", None),
        P(None, "blk", None, None),
        P(),
    )
    return jax.shard_map(
        functools.partial(shards, mesh.shape["blk"], mesh.shape["narrow"]),
        mesh=mesh,
        in_specs=placed,
        out_specs=(P("blk", "narrow"), P(("blk", "narrow"), None, None)),
        check_vma=False,
    )
```

```python
import functools

import jax
import jax.numpy as jnp
from jax import lax
from jax.experimental import pallas as pl
from jax.experimental.pallas import tpu as pltpu
from jax.sharding import PartitionSpec as P

SWEEPS = 8
LEVELS = SWEEPS + 1
OFFSETS = (-2, -1, 1, 2)
LANES = 128
MASS = 2
HOOKS = 6
f32, bf16 = jnp.float32, jnp.bfloat16


def split(x):
    high = x.astype(bf16)
    return high, (x - high.astype(f32)).astype(bf16)


def beside(x):
    return jnp.concatenate(split(x), axis=1)


def below(x):
    return jnp.concatenate(split(x), axis=0)


def product(matrix, field):
    whole = jnp.dot(matrix, field, preferred_element_type=f32)
    rows, cols = whole.shape[0] // 2, whole.shape[1] // 2
    return (whole[:rows, :cols] + whole[:rows, cols:]) + (whole[rows:, :cols] + whole[rows:, cols:])


def kernel(
    count, others, size,
    rhs_hbm, zo_hbm, e_diag_hbm, a_off_hbm, e_off_hbm, col_ref, inv_hbm, shift_ref,
    res_ref, cross_ref,
    far_out, far_in, near_out, near_in, mat_out, mat_in, state_x, state_z, state_n, known,
    base, image, band, by_x, by_n, by_y, by_m, far_x, far_y, inverse, zot, partial, outbox, inbox,
    far_send, far_recv, near_send, near_recv, mat_send, mat_recv, pass_send, pass_recv, cross_send, cross_recv, tokens,
    rhs_ref, zo_ref, e_diag_ref, a_off_ref, e_off_ref, inv_ref, load_sem,
):
    me = lax.axis_index("blk")
    mine = lax.axis_index("narrow")
    devices = count * others
    rank = me * others + mine
    parity = lax.rem(me, 2)
    sign = 1 - 2 * parity
    has_far = jnp.logical_and(me != 0, me != count - 1)
    near_id = me + sign
    far_id = jnp.where(has_far, me - sign, near_id)
    per = outbox.shape[2]
    pair = 2 * size
    quarter = size // 4
    pieces = mat_out.shape[1]
    part = lax.rem(mine, pieces)
    rounds = (count - 2).bit_length()
    short = rounds <= HOOKS

    def row_of(c):
        return c + parity * (3 - 2 * c)

    def rows_of(c):
        return pl.ds(pl.multiple_of(row_of(c) * size, 8), size)

    loads = [
        pltpu.make_async_copy(source, target, load_sem.at[k])
        for k, (source, target) in enumerate((
            (rhs_hbm, rhs_ref), (inv_hbm, inv_ref), (a_off_hbm, a_off_ref), (e_off_hbm, e_off_ref),
            (e_diag_hbm, e_diag_ref), (zo_hbm, zo_ref),
        ))
    ]
    barrier = pltpu.get_barrier_semaphore()
    for load in loads:
        load.start()

    def greet(**where):
        pl.semaphore_signal(barrier, inc=1, device_id=where, device_id_type=pl.DeviceIdType.MESH)

    def everyone(act):
        def at(k, carry):
            b = lax.rem(k + me + count // 2, count)
            for n in range(others):
                @pl.when(jnp.logical_or(b != me, n != mine))
                def _():
                    act(b, n)
            return carry
        lax.fori_loop(0, count, at, 0)

    if short:
        greet(blk=near_id)

        @pl.when(has_far)
        def _():
            greet(blk=far_id)

        for k in range(1, others):
            greet(narrow=lax.rem(mine + k, others))
        greeted = others + jnp.where(has_far, 1, 0)
    else:
        everyone(lambda b, n: greet(blk=b, narrow=n))
        greeted = devices - 1

    @pl.when(jnp.logical_not(has_far))
    def _():
        def clear(s, carry):
            far_in[s] = jnp.zeros((pair, LANES), f32)
            return carry
        lax.fori_loop(0, 2 * LEVELS, clear, 0)
        mat_in[...] = jnp.zeros_like(mat_in)

    def tell(t):
        if not short or t >= rounds:
            return
        d = 1 << t
        for up, there, target in (
            (0, me + d < count, jnp.minimum(me + d, count - 1)),
            (1, me - d >= 0, jnp.maximum(me - d, 0)),
        ):
            @pl.when(there)
            def _():
                pl.semaphore_signal(
                    tokens.at[t, up], inc=1, device_id={"blk": target}, device_id_type=pl.DeviceIdType.MESH
                )

    def hear(t):
        if not short or t >= rounds:
            return
        d = 1 << t
        for up, there in ((0, me - d >= 0), (1, me + d < count)):
            @pl.when(there)
            def _():
                pl.semaphore_wait(tokens.at[t, up], 1)

        tell(t + 1)

    def far_copy(f):
        return pltpu.make_async_remote_copy(
            src_ref=far_out.at[f], dst_ref=far_in.at[f],
            send_sem=far_send.at[f], recv_sem=far_recv.at[f],
            device_id={"blk": far_id}, device_id_type=pl.DeviceIdType.MESH,
        )

    def near_copy(s):
        return pltpu.make_async_remote_copy(
            src_ref=near_out.at[s], dst_ref=near_in.at[s],
            send_sem=near_send.at[s], recv_sem=near_recv.at[s],
            device_id={"blk": near_id}, device_id_type=pl.DeviceIdType.MESH,
        )

    def mat_copy(which):
        return pltpu.make_async_remote_copy(
            src_ref=mat_out.at[which, part], dst_ref=mat_in.at[which, part],
            send_sem=mat_send.at[which], recv_sem=mat_recv.at[which],
            device_id={"blk": far_id}, device_id_type=pl.DeviceIdType.MESH,
        )

    def pass_copy(which):
        return pltpu.make_async_remote_copy(
            src_ref=mat_in.at[which, part], dst_ref=mat_in.at[which, part],
            send_sem=pass_send.at[which], recv_sem=pass_recv.at[which],
            device_id={"narrow": mine + 1 - 2 * lax.rem(mine, 2)}, device_id_type=pl.DeviceIdType.MESH,
        )

    def if_far(act):
        pl.when(has_far)(act)

    def send_far(f, value):
        far_out[f] = value
        if_far(lambda: far_copy(f).start())

    def send_near(s, value):
        near_out[s] = value
        near_copy(s).start()

    def from_far(f):
        if_far(lambda: far_copy(f).wait_recv())
        return far_in[f]

    def from_near(s):
        near_copy(s).wait_recv()
        return near_in[s]

    filler = jnp.zeros((LANES - size, 2 * LANES), bf16)

    def field(value):
        return jnp.concatenate([beside(value[:size]), filler, beside(value[size:]), filler], axis=0)

    def solved(which, c, value):
        return product(inverse[which, c], beside(value))

    def put(matrix, which, row, k, block):
        rows = matrix.shape[1] // 2
        high, low = split(block)
        lanes = slice(k * LANES, (k + 1) * LANES)
        matrix[which, row * size:(row + 1) * size, lanes] = high
        matrix[which, rows + row * size:rows + (row + 1) * size, lanes] = low

    nothing = jnp.zeros((size, LANES), f32)

    def place(which, row, blocks):
        def at(c):
            return blocks[c - row] if c - row in blocks else nothing

        for k in range(2):
            put(by_x, which, row, k, at(k))
            put(by_n, which, row, k, at(2 + k))
            if row < 2:
                put(by_y, which, row, k, at(-1 - k))
            else:
                put(by_m, which, row - 2, k, at(5 - k))

    def build_band(c):
        row = row_of(c)
        for k, offset in enumerate(OFFSETS):
            total_a = jnp.zeros((size, size), f32)
            total_e = jnp.zeros((size, size), f32)
            for s in range(3):
                weight = jnp.where(col_ref[row, s] == me * 4 + row + sign * offset, f32(1.0), f32(0.0))
                total_a = total_a + weight * a_off_ref[row, s]
                total_e = total_e + weight * e_off_ref[row, s]
            band[0, c, :, k * LANES:k * LANES + size] = total_a
            band[1, c, :, k * LANES:k * LANES + size] = total_e

    def pack(block):
        rest = block[3 * quarter:, :size]
        third = size // 3
        return jnp.concatenate([
            jnp.concatenate(
                [block[g * quarter:(g + 1) * quarter, :size], rest[:, g * third:(g + 1) * third]], axis=1
            )
            for g in range(3)
        ], axis=0)

    def unpack(packed):
        groups = [packed[g * quarter:(g + 1) * quarter] for g in range(3)]
        whole = jnp.concatenate(
            [group[:, :size] for group in groups]
            + [jnp.concatenate([group[:, size:] for group in groups], axis=1)],
            axis=0,
        )
        return jnp.concatenate([whole, jnp.zeros((size, LANES - size), f32)], axis=1)

    def spans(j):
        first, stop, share = 3 * quarter * j, 3 * quarter * (j + 1), mat_out.shape[2]
        while first < stop:
            piece = first // share
            end = min(stop, (piece + 1) * share)
            yield piece, first - piece * share, end - piece * share
            first = end

    def build_sweep(which, rows, send=True):
        q = shift_ref[which]
        for c in rows:
            merged = product(inverse[which, c], beside(band[0, c] - q * band[1, c]))
            blocks = {o: merged[:, k * LANES:(k + 1) * LANES] for k, o in enumerate(OFFSETS)}
            for j, offset in {0: ((0, -1), (1, -2), (3, 1)), 1: ((2, -2), (4, -1))}.get(c, ()):
                packed, at = pack(blocks[offset]), 0
                for piece, first, stop in spans(j):
                    mat_out[which, piece, first:stop] = packed[at:at + stop - first]
                    at += stop - first
            if c == 1 and send:
                send_mat(which)
            place(which, c, blocks)

    def send_mat(which):
        if_far(lambda: mat_copy(which).start())

    def pass_mat(which):
        @pl.when(has_far)
        def _():
            mat_copy(which).wait_recv()
            if pieces == 2:
                pass_copy(which).start()

    def build_far(which):
        if pieces == 2:
            if_far(lambda: pass_copy(which).wait_recv())
        blocks = [
            unpack(jnp.concatenate([mat_in[which, p, first:stop] for p, first, stop in spans(j)], axis=0))
            for j in range(5)
        ]
        for matrix, rows in (
            (far_x, ((blocks[0], blocks[1]), (blocks[2], nothing))),
            (far_y, ((nothing, blocks[3]), (blocks[4], nothing))),
        ):
            for row, columns in enumerate(rows):
                for k, block in enumerate(columns):
                    put(matrix, which, row, k, block)

    def build_mass():
        for c in range(4):
            blocks = {o: band[1, c, :, k * LANES:(k + 1) * LANES] for k, o in enumerate(OFFSETS)}
            blocks[0] = jnp.concatenate([e_diag_ref[row_of(c)], jnp.zeros((size, LANES - size), f32)], axis=1)
            place(MASS, c, blocks)

    def level(which, k, last=False, late=None, skip=False, aside=None):
        f = which * LEVELS + k
        if aside is not None:
            aside()
        fx = field(state_x[...])
        gx = product(by_x[which], fx)
        n = (state_n[...] - gx[pair:]) - product(by_m[which], field(from_near(f)))
        send_near(f + 1, n)
        fn = field(n)
        if not last:
            gn = product(by_n[which], fn)
            free = base[0] - gn[:pair]
            if which or not (skip or late):
                send_far(f + 2, free)
            state_n[...] = base[1] - gn[pair:]
        if late is not None:
            late()
            if which == 0:
                send_far(f + 2, free)
        if skip:
            y = from_far(f)
        else:
            y = from_far(f) - known[...]
        if which == 0 and skip:
            send_far(f + 2, free)
        fy = field(y)
        x = (state_z[...] - gx[:pair]) - product(by_y[which], fy)
        if not skip:
            known[...] = product(far_y[which], fy) + product(far_x[which], fx)
        if not last:
            state_x[...] = x
            state_z[...] = free
            return None
        gx = product(by_x[MASS], field(x))
        gn = product(by_n[MASS], fn)
        at_n = (gx[pair:] + gn[pair:]) + product(by_m[MASS], field(from_near(f + 1)))

        def at_x():
            y = from_far(f + 1) - known[...]
            return (gx[:pair] + gn[:pair]) + product(by_y[MASS], field(y))

        return at_n, at_x

    def begin_field(which):
        gn = product(by_n[which], field(base[1]))
        free = base[0] - gn[:pair]
        send_far(which * LEVELS + 1, free)
        state_x[...] = base[0]
        state_z[...] = free
        state_n[...] = base[1] - gn[pair:]

    def start_with(which, half, values):
        for k, value in enumerate(values):
            base[half, k * size:(k + 1) * size] = solved(which, 2 * half + k, value)

    loads[0].wait()
    loads[1].wait()
    for c in range(4):
        inverse[0, c] = below(inv_ref[0, row_of(c)])
    for half in range(2):
        start_with(0, half, [rhs_ref[rows_of(2 * half + k), :] for k in range(2)])
    pl.semaphore_wait(barrier, greeted)
    send_far(0, base[0])
    send_near(0, base[1])
    tell(0)
    band[...] = jnp.zeros_like(band)
    for load in loads[2:]:
        load.wait()
    for half in range(2):
        for c in (2 * half, 2 * half + 1):
            build_band(c)
        build_sweep(0, (2 * half, 2 * half + 1))

    def post(which):
        def act(b, n):
            pltpu.make_async_remote_copy(
                src_ref=outbox.at[which, b * others + n],
                dst_ref=inbox.at[which, rank],
                send_sem=cross_send.at[which],
                recv_sem=cross_recv.at[which],
                device_id={"blk": b, "narrow": n},
                device_id_type=pl.DeviceIdType.MESH,
            ).start()

        everyone(act)

    def late(which):
        if which == 0:
            pass_mat(which)
        else:
            hear(2)
        build_far(which)
        f = which * LEVELS
        known[...] = product(far_y[which], field(far_in[f])) + product(far_x[which], field(far_out[f]))

    def mass_aside():
        for c in range(4):
            inverse[1, c] = below(inv_ref[1, row_of(c)])
        build_mass()

    def sweep_aside():
        hear(0)
        build_sweep(1, range(4), send=False)
        zot[...] = below(zo_ref[...])

    def mat_aside():
        send_mat(1)
        hear(1)

    def post_aside():
        for t in range(3, HOOKS):
            hear(t)
        post(0)

    for which in range(2):
        begin_field(which)
        level(which, 0, skip=True)
        level(which, 1, late=functools.partial(late, which))
        if which == 0:
            level(which, 2, aside=mass_aside)
            level(which, 3, aside=sweep_aside)
        then = 2 if which else 4

        def step(k, carry):
            level(which, k)
            return carry

        lax.fori_loop(then, SWEEPS - 1, step, 0)
        at_n, at_x = level(which, SWEEPS - 1, last=True, aside=post_aside if which else mat_aside)

        q = shift_ref[which]
        root = jnp.sqrt(jnp.full((1, LANES), 2.0 * q, f32))
        for half, value in ((1, at_n), (0, at_x())):
            after = []
            for k in range(2):
                mass = value[k * size:(k + 1) * size]
                rows = rows_of(2 * half + k)
                before = rhs_ref[rows, :] if which == 0 else res_ref[rows, :]
                after.append(before + (2.0 * q) * mass)
                res_ref[rows, :] = after[k]
                image[rows, :] = root * mass
            if which == 0:
                start_with(1, half, after)
                if half == 1:
                    send_near(LEVELS, base[1])
                else:
                    send_far(LEVELS, base[0])
        if which == 0:
            pass_mat(1)

        partial[...] = product(zot[...], beside(image[...]))

        def deal(d, carry):
            outbox[which, d] = partial[pl.ds(d * per, per), :]
            return carry

        lax.fori_loop(0, devices, deal, 0, unroll=8)

        if which == 1:
            post(1)
        inbox[which, rank] = outbox[which, rank]

    @pl.when(has_far)
    def _():
        def settle(f, carry):
            far_copy(f).wait_send()
            return carry
        lax.fori_loop(0, 2 * LEVELS, settle, 0)
        for which in range(2):
            mat_copy(which).wait_send()
            if pieces == 2:
                pass_copy(which).wait_send()

    def settle_near(s, carry):
        near_copy(s).wait_send()
        return carry

    lax.fori_loop(0, 2 * LEVELS, settle_near, 0)

    for which in range(2):
        most = pl.ds(0, devices - 1)
        pltpu.make_async_copy(outbox.at[which, most], inbox.at[which, most], cross_recv.at[which]).wait()
        for n in range(others):
            total = inbox[which, n]
            for b in range(1, count):
                total = total + inbox[which, b * others + n]
            cross_ref[:, which, n * LANES:(n + 1) * LANES] = total
        pltpu.make_async_copy(outbox.at[which, most], inbox.at[which, most], cross_send.at[which]).wait()


def shards(count, others, rhs, zo, e_diag, a_off, e_off, col_index, inv_diag, shifts):
    row_count, col_width = rhs.shape
    size = e_diag.shape[1]
    ko = zo.shape[1]
    devices = count * others
    per = ko // devices
    assert row_count == 4 * size and col_width == LANES and count % 2 == 0
    vmem = pl.BlockSpec(memory_space=pltpu.VMEM)
    smem = pl.BlockSpec(memory_space=pltpu.SMEM)
    hbm = pl.BlockSpec(memory_space=pl.ANY)
    pair = 2 * size
    width = 2 * LANES
    pieces = 2 - others % 2
    share = -(-5 * 3 * (size // 4) // (8 * pieces)) * 8
    return pl.pallas_call(
        functools.partial(kernel, count, others, size),
        out_shape=(
            pltpu.VMEM((row_count, col_width), f32),
            pltpu.VMEM((per, 2, others * LANES), f32),
        ),
        in_specs=[hbm, hbm, hbm, hbm, hbm, smem, hbm, smem],
        out_specs=(vmem, vmem),
        scratch_shapes=[
            pltpu.VMEM((2 * LEVELS, pair, LANES), f32),
            pltpu.VMEM((2 * LEVELS, pair, LANES), f32),
            pltpu.VMEM((2 * LEVELS, pair, LANES), f32),
            pltpu.VMEM((2 * LEVELS, pair, LANES), f32),
            pltpu.VMEM((2, pieces, share, LANES), f32),
            pltpu.VMEM((2, pieces, share, LANES), f32),
            *(pltpu.VMEM((pair, LANES), f32) for _ in range(4)),
            pltpu.VMEM((2, pair, LANES), f32),
            pltpu.VMEM((row_count, LANES), f32),
            pltpu.VMEM((2, 4, size, 4 * LANES), f32),
            pltpu.VMEM((3, 4 * pair, width), bf16),
            pltpu.VMEM((3, 4 * pair, width), bf16),
            pltpu.VMEM((3, 2 * pair, width), bf16),
            pltpu.VMEM((3, 2 * pair, width), bf16),
            pltpu.VMEM((2, 2 * pair, width), bf16),
            pltpu.VMEM((2, 2 * pair, width), bf16),
            pltpu.VMEM((2, 4, 2 * size, size), bf16),
            pltpu.VMEM((2 * ko, row_count), bf16),
            pltpu.VMEM((ko, LANES), f32),
            pltpu.VMEM((2, devices, per, LANES), f32),
            pltpu.VMEM((2, devices, per, LANES), f32),
            pltpu.SemaphoreType.DMA((2 * LEVELS,)),
            pltpu.SemaphoreType.DMA((2 * LEVELS,)),
            pltpu.SemaphoreType.DMA((2 * LEVELS,)),
            pltpu.SemaphoreType.DMA((2 * LEVELS,)),
            pltpu.SemaphoreType.DMA((2,)),
            pltpu.SemaphoreType.DMA((2,)),
            pltpu.SemaphoreType.DMA((2,)),
            pltpu.SemaphoreType.DMA((2,)),
            pltpu.SemaphoreType.DMA((2,)),
            pltpu.SemaphoreType.DMA((2,)),
            pltpu.SemaphoreType.REGULAR((HOOKS, 2)),
            *(pltpu.VMEM(x.shape, f32) for x in (rhs, zo.T, e_diag, a_off, e_off, inv_diag)),
            pltpu.SemaphoreType.DMA((6,)),
        ],
        compiler_params=pltpu.CompilerParams(
            collective_id=0, has_side_effects=True
        ),
    )(rhs, zo.T, e_diag, a_off, e_off, col_index, inv_diag, shifts)


def solution(mesh):
    placed = (
        P("blk", "narrow"),
        P("blk", None),
        P("blk", None, None),
        P("blk", None, None, None),
        P("blk", None, None, None),
        P("blk", None),
        P(None, "blk", None, None),
        P(),
    )
    return jax.shard_map(
        functools.partial(shards, mesh.shape["blk"], mesh.shape["narrow"]),
        mesh=mesh,
        in_specs=placed,
        out_specs=(P("blk", "narrow"), P(("blk", "narrow"), None, None)),
        check_vma=False,
    )
```

```python
import functools

import jax
import jax.numpy as jnp
from jax import lax
from jax.experimental import pallas as pl
from jax.experimental.pallas import tpu as pltpu
from jax.sharding import PartitionSpec as P

SWEEPS = 8
LEVELS = SWEEPS + 1
OFFSETS = (-2, -1, 1, 2)
LANES = 128
MASS = 2
HOOKS = 6
f32, bf16 = jnp.float32, jnp.bfloat16


def split(x):
    high = x.astype(bf16)
    return high, (x - high.astype(f32)).astype(bf16)


def beside(x):
    return jnp.concatenate(split(x), axis=1)


def below(x):
    return jnp.concatenate(split(x), axis=0)


def product(matrix, field):
    whole = jnp.dot(matrix, field, preferred_element_type=f32)
    rows, cols = whole.shape[0] // 2, whole.shape[1] // 2
    return (whole[:rows, :cols] + whole[:rows, cols:]) + (whole[rows:, :cols] + whole[rows:, cols:])


def kernel(
    count, others, size,
    rhs_hbm, zo_hbm, e_diag_hbm, a_off_hbm, e_off_hbm, col_ref, inv_hbm, shift_ref,
    res_ref, cross_ref,
    far_out, far_in, near_out, near_in, mat_out, mat_in, mix_out, mix_in, state_x, state_z, state_n, known,
    base, image, band, by_x, by_n, by_y, by_m, far_x, far_y, inverse, zot, partial, outbox, inbox,
    far_send, far_recv, near_send, near_recv, mat_send, mat_recv, pass_send, pass_recv, cross_send, cross_recv, mix_send, mix_recv, tokens,
    rhs_ref, zo_ref, e_diag_ref, a_off_ref, e_off_ref, inv_ref, load_sem,
):
    me = lax.axis_index("blk")
    mine = lax.axis_index("narrow")
    devices = count * others
    rank = me * others + mine
    parity = lax.rem(me, 2)
    sign = 1 - 2 * parity
    has_far = jnp.logical_and(me != 0, me != count - 1)
    near_id = me + sign
    far_id = jnp.where(has_far, me - sign, near_id)
    per = outbox.shape[2]
    pair = 2 * size
    quarter = size // 4
    pieces = mat_out.shape[1]
    part = lax.rem(mine, pieces)
    rounds = (count - 2).bit_length()
    short = rounds <= HOOKS

    def row_of(c):
        return c + parity * (3 - 2 * c)

    def rows_of(c):
        return pl.ds(pl.multiple_of(row_of(c) * size, 8), size)

    loads = [
        pltpu.make_async_copy(source, target, load_sem.at[k])
        for k, (source, target) in enumerate((
            (rhs_hbm, rhs_ref), (inv_hbm, inv_ref), (a_off_hbm, a_off_ref), (e_off_hbm, e_off_ref),
            (e_diag_hbm, e_diag_ref), (zo_hbm, zo_ref),
        ))
    ]
    barrier = pltpu.get_barrier_semaphore()
    for load in loads:
        load.start()

    def greet(**where):
        pl.semaphore_signal(barrier, inc=1, device_id=where, device_id_type=pl.DeviceIdType.MESH)

    def everyone(act):
        def at(k, carry):
            b = lax.rem(k + me + count // 2, count)
            for n in range(others):
                @pl.when(jnp.logical_or(b != me, n != mine))
                def _():
                    act(b, n)
            return carry
        lax.fori_loop(0, count, at, 0)

    if short:
        greet(blk=near_id)

        @pl.when(has_far)
        def _():
            greet(blk=far_id)

        for k in range(1, others):
            greet(narrow=lax.rem(mine + k, others))
        greeted = others + jnp.where(has_far, 1, 0)
    else:
        everyone(lambda b, n: greet(blk=b, narrow=n))
        greeted = devices - 1

    @pl.when(jnp.logical_not(has_far))
    def _():
        def clear(s, carry):
            far_in[s] = jnp.zeros((pair, LANES), f32)
            return carry
        lax.fori_loop(0, 2 * LEVELS, clear, 0)
        mat_in[...] = jnp.zeros_like(mat_in)
        mix_in[...] = jnp.zeros_like(mix_in)

    def tell(t):
        if not short or t >= rounds:
            return
        d = 1 << t
        for up, there, target in (
            (0, me + d < count, jnp.minimum(me + d, count - 1)),
            (1, me - d >= 0, jnp.maximum(me - d, 0)),
        ):
            @pl.when(there)
            def _():
                pl.semaphore_signal(
                    tokens.at[t, up], inc=1, device_id={"blk": target}, device_id_type=pl.DeviceIdType.MESH
                )

    def hear(t):
        if not short or t >= rounds:
            return
        d = 1 << t
        for up, there in ((0, me - d >= 0), (1, me + d < count)):
            @pl.when(there)
            def _():
                pl.semaphore_wait(tokens.at[t, up], 1)

        tell(t + 1)

    def far_copy(f):
        return pltpu.make_async_remote_copy(
            src_ref=far_out.at[f], dst_ref=far_in.at[f],
            send_sem=far_send.at[f], recv_sem=far_recv.at[f],
            device_id={"blk": far_id}, device_id_type=pl.DeviceIdType.MESH,
        )

    def near_copy(s):
        return pltpu.make_async_remote_copy(
            src_ref=near_out.at[s], dst_ref=near_in.at[s],
            send_sem=near_send.at[s], recv_sem=near_recv.at[s],
            device_id={"blk": near_id}, device_id_type=pl.DeviceIdType.MESH,
        )

    def mat_copy(which):
        return pltpu.make_async_remote_copy(
            src_ref=mat_out.at[which, part], dst_ref=mat_in.at[which, part],
            send_sem=mat_send.at[which], recv_sem=mat_recv.at[which],
            device_id={"blk": far_id}, device_id_type=pl.DeviceIdType.MESH,
        )

    def mix_copy():
        return pltpu.make_async_remote_copy(
            src_ref=mix_out, dst_ref=mix_in, send_sem=mix_send, recv_sem=mix_recv,
            device_id={"blk": far_id}, device_id_type=pl.DeviceIdType.MESH,
        )

    def pass_copy(which):
        return pltpu.make_async_remote_copy(
            src_ref=mat_in.at[which, part], dst_ref=mat_in.at[which, part],
            send_sem=pass_send.at[which], recv_sem=pass_recv.at[which],
            device_id={"narrow": mine + 1 - 2 * lax.rem(mine, 2)}, device_id_type=pl.DeviceIdType.MESH,
        )

    def if_far(act):
        pl.when(has_far)(act)

    def send_far(f, value):
        far_out[f] = value
        if_far(lambda: far_copy(f).start())

    def send_near(s, value):
        near_out[s] = value
        near_copy(s).start()

    def from_far(f):
        if_far(lambda: far_copy(f).wait_recv())
        return far_in[f]

    def from_near(s):
        near_copy(s).wait_recv()
        return near_in[s]

    filler = jnp.zeros((LANES - size, 2 * LANES), bf16)

    def field(value):
        return jnp.concatenate([beside(value[:size]), filler, beside(value[size:]), filler], axis=0)

    def solved(which, c, value):
        return product(inverse[which, c], beside(value))

    def put(matrix, which, row, k, block):
        rows = matrix.shape[1] // 2
        high, low = split(block)
        lanes = slice(k * LANES, (k + 1) * LANES)
        matrix[which, row * size:(row + 1) * size, lanes] = high
        matrix[which, rows + row * size:rows + (row + 1) * size, lanes] = low

    nothing = jnp.zeros((size, LANES), f32)

    def place(which, row, blocks):
        def at(c):
            return blocks[c - row] if c - row in blocks else nothing

        for k in range(2):
            put(by_x, which, row, k, at(k))
            put(by_n, which, row, k, at(2 + k))
            if row < 2:
                put(by_y, which, row, k, at(-1 - k))
            else:
                put(by_m, which, row - 2, k, at(5 - k))

    def build_band(c):
        row = row_of(c)
        for k, offset in enumerate(OFFSETS):
            total_a = jnp.zeros((size, size), f32)
            total_e = jnp.zeros((size, size), f32)
            for s in range(3):
                weight = jnp.where(col_ref[row, s] == me * 4 + row + sign * offset, f32(1.0), f32(0.0))
                total_a = total_a + weight * a_off_ref[row, s]
                total_e = total_e + weight * e_off_ref[row, s]
            band[0, c, :, k * LANES:k * LANES + size] = total_a
            band[1, c, :, k * LANES:k * LANES + size] = total_e

    def pack(block):
        rest = block[3 * quarter:, :size]
        third = size // 3
        return jnp.concatenate([
            jnp.concatenate(
                [block[g * quarter:(g + 1) * quarter, :size], rest[:, g * third:(g + 1) * third]], axis=1
            )
            for g in range(3)
        ], axis=0)

    def unpack(packed):
        groups = [packed[g * quarter:(g + 1) * quarter] for g in range(3)]
        whole = jnp.concatenate(
            [group[:, :size] for group in groups]
            + [jnp.concatenate([group[:, size:] for group in groups], axis=1)],
            axis=0,
        )
        return jnp.concatenate([whole, jnp.zeros((size, LANES - size), f32)], axis=1)

    def spans(j):
        first, stop, share = 3 * quarter * j, 3 * quarter * (j + 1), mat_out.shape[2]
        while first < stop:
            piece = first // share
            end = min(stop, (piece + 1) * share)
            yield piece, first - piece * share, end - piece * share
            first = end

    def build_sweep(which, rows, send=True):
        q = shift_ref[which]
        for c in rows:
            merged = product(inverse[which, c], beside(band[0, c] - q * band[1, c]))
            blocks = {o: merged[:, k * LANES:(k + 1) * LANES] for k, o in enumerate(OFFSETS)}
            for j, offset in {0: ((0, -1), (1, -2), (3, 1)), 1: ((2, -2), (4, -1))}.get(c, ()):
                packed, at = pack(blocks[offset]), 0
                for piece, first, stop in spans(j):
                    mat_out[which, piece, first:stop] = packed[at:at + stop - first]
                    at += stop - first
            if c == 1 and send:
                send_mat(which)
            place(which, c, blocks)

    def send_mat(which):
        if_far(lambda: mat_copy(which).start())

    def pass_mat(which):
        @pl.when(has_far)
        def _():
            mat_copy(which).wait_recv()
            if pieces == 2:
                pass_copy(which).start()

    def build_far(which):
        if pieces == 2:
            if_far(lambda: pass_copy(which).wait_recv())
        blocks = [
            unpack(jnp.concatenate([mat_in[which, p, first:stop] for p, first, stop in spans(j)], axis=0))
            for j in range(5)
        ]
        for matrix, rows in (
            (far_x, ((blocks[0], blocks[1]), (blocks[2], nothing))),
            (far_y, ((nothing, blocks[3]), (blocks[4], nothing))),
        ):
            for row, columns in enumerate(rows):
                for k, block in enumerate(columns):
                    put(matrix, which, row, k, block)

    def build_mass():
        for c in range(4):
            blocks = {o: band[1, c, :, k * LANES:(k + 1) * LANES] for k, o in enumerate(OFFSETS)}
            blocks[0] = jnp.concatenate([e_diag_ref[row_of(c)], jnp.zeros((size, LANES - size), f32)], axis=1)
            place(MASS, c, blocks)

    def level(which, k, last=False, late=None, skip=False, aside=None):
        f = which * LEVELS + k
        if aside is not None:
            aside()
        fx = field(state_x[...])
        gx = product(by_x[which], fx)
        n = (state_n[...] - gx[pair:]) - product(by_m[which], field(from_near(f)))
        send_near(f + 1, n)
        fn = field(n)
        if not last:
            gn = product(by_n[which], fn)
            free = base[0] - gn[:pair]
            if which or not (skip or late):
                send_far(f + 2, free)
            state_n[...] = base[1] - gn[pair:]
        if late is not None:
            late()
            if which == 0:
                send_far(f + 2, free)
        if skip:
            y = from_far(f)
        else:
            y = from_far(f) - known[...]
        if which == 0 and skip:
            send_far(f + 2, free)
        fy = field(y)
        x = (state_z[...] - gx[:pair]) - product(by_y[which], fy)
        if not skip:
            known[...] = product(far_y[which], fy) + product(far_x[which], fx)
        if not last:
            state_x[...] = x
            state_z[...] = free
            return None
        fx_last = field(x)
        gx = product(by_x[MASS], fx_last)
        gn = product(by_n[MASS], fn)
        at_n = (gx[pair:] + gn[pair:]) + product(by_m[MASS], field(from_near(f + 1)))

        def at_x():
            y = from_far(f + 1) - known[...]
            return (gx[:pair] + gn[:pair]) + product(by_y[MASS], field(y))

        return at_n, gx[:pair] + gn[:pair], fx_last, at_x

    def begin_field(which):
        gn = product(by_n[which], field(base[1]))
        free = base[0] - gn[:pair]
        send_far(which * LEVELS + 1, free)
        state_x[...] = base[0]
        state_z[...] = free
        state_n[...] = base[1] - gn[pair:]

    def start_with(which, half, values):
        for k, value in enumerate(values):
            base[half, k * size:(k + 1) * size] = solved(which, 2 * half + k, value)

    loads[0].wait()
    loads[1].wait()
    for c in range(4):
        inverse[0, c] = below(inv_ref[0, row_of(c)])
    for half in range(2):
        start_with(0, half, [rhs_ref[rows_of(2 * half + k), :] for k in range(2)])
    pl.semaphore_wait(barrier, greeted)
    send_far(0, base[0])
    send_near(0, base[1])
    tell(0)
    band[...] = jnp.zeros_like(band)
    for load in loads[2:]:
        load.wait()
    for half in range(2):
        for c in (2 * half, 2 * half + 1):
            build_band(c)
        build_sweep(0, (2 * half, 2 * half + 1))

    def post(which):
        def act(b, n):
            pltpu.make_async_remote_copy(
                src_ref=outbox.at[which, b * others + n],
                dst_ref=inbox.at[which, rank],
                send_sem=cross_send.at[which],
                recv_sem=cross_recv.at[which],
                device_id={"blk": b, "narrow": n},
                device_id_type=pl.DeviceIdType.MESH,
            ).start()

        everyone(act)

    def build_mix():
        weights = [
            below(jnp.where(
                parity == 0, zo_ref[:, c * size:(c + 1) * size], zo_ref[:, (3 - c) * size:(4 - c) * size]
            ))
            for c in range(2)
        ]
        blocks = [[band[1, c, :, k * LANES:(k + 1) * LANES] for k in (1, 0)] for c in range(2)]
        mix_out[0] = product(weights[0], beside(blocks[0][0])) + product(weights[1], beside(blocks[1][1]))
        mix_out[1] = product(weights[0], beside(blocks[0][1]))

    def late(which):
        if which == 0:
            build_mix()
            pass_mat(which)
            if_far(lambda: mix_copy().start())
        else:
            hear(2)
        build_far(which)
        f = which * LEVELS
        known[...] = product(far_y[which], field(far_in[f])) + product(far_x[which], field(far_out[f]))

    def mass_aside():
        for c in range(4):
            inverse[1, c] = below(inv_ref[1, row_of(c)])
        build_mass()

    def sweep_aside():
        hear(0)
        build_sweep(1, range(4), send=False)
        zot[...] = below(zo_ref[...])

    def mat_aside():
        send_mat(1)
        hear(1)

    def post_aside():
        for t in range(3, HOOKS):
            hear(t)
        post(0)

    def deal(which):
        def at(d, carry):
            outbox[which, d] = partial[pl.ds(d * per, per), :]
            return carry

        lax.fori_loop(0, devices, at, 0, unroll=8)

    for which in range(2):
        begin_field(which)
        level(which, 0, skip=True)
        level(which, 1, late=functools.partial(late, which))
        if which == 0:
            level(which, 2, aside=mass_aside)
            level(which, 3, aside=sweep_aside)
        then = 2 if which else 4

        def step(k, carry):
            level(which, k)
            return carry

        lax.fori_loop(then, SWEEPS - 1, step, 0)
        at_n, ahead, fx, at_x = level(which, SWEEPS - 1, last=True, aside=post_aside if which else mat_aside)

        q = shift_ref[which]
        root = jnp.sqrt(jnp.full((1, LANES), 2.0 * q, f32))
        if which == 1:
            if_far(lambda: mix_copy().wait_recv())
            for half, value in ((1, at_n), (0, ahead)):
                for k in range(2):
                    image[rows_of(2 * half + k), :] = root * value[k * size:(k + 1) * size]
            mixed = below(jnp.concatenate([mix_in[0], mix_in[1]], axis=1))
            partial[...] = product(zot[...], beside(image[...])) + root * product(mixed, fx)
            deal(1)
            post(1)
            inbox[1, rank] = outbox[1, rank]

        for half in (1, 0):
            value = at_n if half else at_x()
            after = []
            for k in range(2):
                mass = value[k * size:(k + 1) * size]
                rows = rows_of(2 * half + k)
                before = rhs_ref[rows, :] if which == 0 else res_ref[rows, :]
                after.append(before + (2.0 * q) * mass)
                res_ref[rows, :] = after[k]
                if which == 0:
                    image[rows, :] = root * mass
            if which == 0:
                start_with(1, half, after)
                if half == 1:
                    send_near(LEVELS, base[1])
                else:
                    send_far(LEVELS, base[0])
        if which == 0:
            pass_mat(1)
            partial[...] = product(zot[...], beside(image[...]))
            deal(0)
            inbox[0, rank] = outbox[0, rank]

    @pl.when(has_far)
    def _():
        def settle(f, carry):
            far_copy(f).wait_send()
            return carry
        lax.fori_loop(0, 2 * LEVELS, settle, 0)
        mix_copy().wait_send()
        for which in range(2):
            mat_copy(which).wait_send()
            if pieces == 2:
                pass_copy(which).wait_send()

    def settle_near(s, carry):
        near_copy(s).wait_send()
        return carry

    lax.fori_loop(0, 2 * LEVELS, settle_near, 0)

    for which in range(2):
        most = pl.ds(0, devices - 1)
        pltpu.make_async_copy(outbox.at[which, most], inbox.at[which, most], cross_recv.at[which]).wait()
        for n in range(others):
            total = inbox[which, n]
            for b in range(1, count):
                total = total + inbox[which, b * others + n]
            cross_ref[:, which, n * LANES:(n + 1) * LANES] = total
        pltpu.make_async_copy(outbox.at[which, most], inbox.at[which, most], cross_send.at[which]).wait()


def shards(count, others, rhs, zo, e_diag, a_off, e_off, col_index, inv_diag, shifts):
    row_count, col_width = rhs.shape
    size = e_diag.shape[1]
    ko = zo.shape[1]
    devices = count * others
    per = ko // devices
    assert row_count == 4 * size and col_width == LANES and count % 2 == 0
    vmem = pl.BlockSpec(memory_space=pltpu.VMEM)
    smem = pl.BlockSpec(memory_space=pltpu.SMEM)
    hbm = pl.BlockSpec(memory_space=pl.ANY)
    pair = 2 * size
    width = 2 * LANES
    pieces = 2 - others % 2
    share = -(-5 * 3 * (size // 4) // (8 * pieces)) * 8
    return pl.pallas_call(
        functools.partial(kernel, count, others, size),
        out_shape=(
            pltpu.VMEM((row_count, col_width), f32),
            pltpu.VMEM((per, 2, others * LANES), f32),
        ),
        in_specs=[hbm, hbm, hbm, hbm, hbm, smem, hbm, smem],
        out_specs=(vmem, vmem),
        scratch_shapes=[
            pltpu.VMEM((2 * LEVELS, pair, LANES), f32),
            pltpu.VMEM((2 * LEVELS, pair, LANES), f32),
            pltpu.VMEM((2 * LEVELS, pair, LANES), f32),
            pltpu.VMEM((2 * LEVELS, pair, LANES), f32),
            pltpu.VMEM((2, pieces, share, LANES), f32),
            pltpu.VMEM((2, pieces, share, LANES), f32),
            pltpu.VMEM((2, ko, LANES), f32),
            pltpu.VMEM((2, ko, LANES), f32),
            *(pltpu.VMEM((pair, LANES), f32) for _ in range(4)),
            pltpu.VMEM((2, pair, LANES), f32),
            pltpu.VMEM((row_count, LANES), f32),
            pltpu.VMEM((2, 4, size, 4 * LANES), f32),
            pltpu.VMEM((3, 4 * pair, width), bf16),
            pltpu.VMEM((3, 4 * pair, width), bf16),
            pltpu.VMEM((3, 2 * pair, width), bf16),
            pltpu.VMEM((3, 2 * pair, width), bf16),
            pltpu.VMEM((2, 2 * pair, width), bf16),
            pltpu.VMEM((2, 2 * pair, width), bf16),
            pltpu.VMEM((2, 4, 2 * size, size), bf16),
            pltpu.VMEM((2 * ko, row_count), bf16),
            pltpu.VMEM((ko, LANES), f32),
            pltpu.VMEM((2, devices, per, LANES), f32),
            pltpu.VMEM((2, devices, per, LANES), f32),
            pltpu.SemaphoreType.DMA((2 * LEVELS,)),
            pltpu.SemaphoreType.DMA((2 * LEVELS,)),
            pltpu.SemaphoreType.DMA((2 * LEVELS,)),
            pltpu.SemaphoreType.DMA((2 * LEVELS,)),
            pltpu.SemaphoreType.DMA((2,)),
            pltpu.SemaphoreType.DMA((2,)),
            pltpu.SemaphoreType.DMA((2,)),
            pltpu.SemaphoreType.DMA((2,)),
            pltpu.SemaphoreType.DMA((2,)),
            pltpu.SemaphoreType.DMA((2,)),
            pltpu.SemaphoreType.DMA,
            pltpu.SemaphoreType.DMA,
            pltpu.SemaphoreType.REGULAR((HOOKS, 2)),
            *(pltpu.VMEM(x.shape, f32) for x in (rhs, zo.T, e_diag, a_off, e_off, inv_diag)),
            pltpu.SemaphoreType.DMA((6,)),
        ],
        compiler_params=pltpu.CompilerParams(
            collective_id=0, has_side_effects=True
        ),
    )(rhs, zo.T, e_diag, a_off, e_off, col_index, inv_diag, shifts)


def solution(mesh):
    placed = (
        P("blk", "narrow"),
        P("blk", None),
        P("blk", None, None),
        P("blk", None, None, None),
        P("blk", None, None, None),
        P("blk", None),
        P(None, "blk", None, None),
        P(),
    )
    return jax.shard_map(
        functools.partial(shards, mesh.shape["blk"], mesh.shape["narrow"]),
        mesh=mesh,
        in_specs=placed,
        out_specs=(P("blk", "narrow"), P(("blk", "narrow"), None, None)),
        check_vma=False,
    )
```

```python
import functools

import jax
import jax.numpy as jnp
from jax import lax
from jax.experimental import pallas as pl
from jax.experimental.pallas import tpu as pltpu
from jax.sharding import PartitionSpec as P

SWEEPS = 8
LEVELS = SWEEPS + 1
OFFSETS = (-2, -1, 1, 2)
LANES = 128
MASS = 2
HOOKS = 6
f32, bf16 = jnp.float32, jnp.bfloat16


def split(x):
    high = x.astype(bf16)
    return high, (x - high.astype(f32)).astype(bf16)


def beside(x):
    return jnp.concatenate(split(x), axis=1)


def below(x):
    return jnp.concatenate(split(x), axis=0)


def product(matrix, field):
    whole = jnp.dot(matrix, field, preferred_element_type=f32)
    rows, cols = whole.shape[0] // 2, whole.shape[1] // 2
    return (whole[:rows, :cols] + whole[:rows, cols:]) + (whole[rows:, :cols] + whole[rows:, cols:])


def kernel(
    count, others, size,
    rhs_hbm, zo_hbm, e_diag_hbm, a_off_hbm, e_off_hbm, col_ref, inv_hbm, shift_ref,
    res_ref, cross_ref,
    far_out, far_in, near_out, near_in, mat_out, mat_in, mix_out, mix_in, state_x, state_z, state_n, known,
    base, image, band, by_x, by_n, by_y, by_m, far_x, far_y, inverse, zot, partial, outbox, inbox,
    far_send, far_recv, near_send, near_recv, mat_send, mat_recv, pass_send, pass_recv, cross_send, cross_recv, mix_send, mix_recv, tokens,
    rhs_ref, zo_ref, e_diag_ref, a_off_ref, e_off_ref, inv_ref, load_sem,
):
    me = lax.axis_index("blk")
    mine = lax.axis_index("narrow")
    devices = count * others
    rank = me * others + mine
    parity = lax.rem(me, 2)
    sign = 1 - 2 * parity
    has_far = jnp.logical_and(me != 0, me != count - 1)
    near_id = me + sign
    far_id = jnp.where(has_far, me - sign, near_id)
    per = outbox.shape[2]
    pair = 2 * size
    quarter = size // 4
    pieces = mat_out.shape[1]
    part = lax.rem(mine, pieces)
    rounds = (count - 2).bit_length()
    short = rounds <= HOOKS

    def row_of(c):
        return c + parity * (3 - 2 * c)

    def rows_of(c):
        return pl.ds(pl.multiple_of(row_of(c) * size, 8), size)

    loads = [
        pltpu.make_async_copy(source, target, load_sem.at[k])
        for k, (source, target) in enumerate((
            (rhs_hbm, rhs_ref), (inv_hbm, inv_ref), (a_off_hbm, a_off_ref), (e_off_hbm, e_off_ref),
            (e_diag_hbm, e_diag_ref), (zo_hbm, zo_ref),
        ))
    ]
    barrier = pltpu.get_barrier_semaphore()
    for load in loads[:2]:
        load.start()

    def greet(**where):
        pl.semaphore_signal(barrier, inc=1, device_id=where, device_id_type=pl.DeviceIdType.MESH)

    def everyone(act):
        def at(k, carry):
            b = lax.rem(k + me + count // 2, count)
            for n in range(others):
                @pl.when(jnp.logical_or(b != me, n != mine))
                def _():
                    act(b, n)
            return carry
        lax.fori_loop(0, count, at, 0)

    if short:
        greet(blk=near_id)

        @pl.when(has_far)
        def _():
            greet(blk=far_id)

        for k in range(1, others):
            greet(narrow=lax.rem(mine + k, others))
        greeted = others + jnp.where(has_far, 1, 0)
    else:
        everyone(lambda b, n: greet(blk=b, narrow=n))
        greeted = devices - 1

    @pl.when(jnp.logical_not(has_far))
    def _():
        def clear(s, carry):
            far_in[s] = jnp.zeros((pair, LANES), f32)
            return carry
        lax.fori_loop(0, 2 * LEVELS, clear, 0)
        mat_in[...] = jnp.zeros_like(mat_in)
        mix_in[...] = jnp.zeros_like(mix_in)

    def tell(t):
        if not short or t >= rounds:
            return
        d = 1 << t
        for up, there, target in (
            (0, me + d < count, jnp.minimum(me + d, count - 1)),
            (1, me - d >= 0, jnp.maximum(me - d, 0)),
        ):
            @pl.when(there)
            def _():
                pl.semaphore_signal(
                    tokens.at[t, up], inc=1, device_id={"blk": target}, device_id_type=pl.DeviceIdType.MESH
                )

    def hear(t):
        if not short or t >= rounds:
            return
        d = 1 << t
        for up, there in ((0, me - d >= 0), (1, me + d < count)):
            @pl.when(there)
            def _():
                pl.semaphore_wait(tokens.at[t, up], 1)

        tell(t + 1)

    def far_copy(f):
        return pltpu.make_async_remote_copy(
            src_ref=far_out.at[f], dst_ref=far_in.at[f],
            send_sem=far_send.at[f], recv_sem=far_recv.at[f],
            device_id={"blk": far_id}, device_id_type=pl.DeviceIdType.MESH,
        )

    def near_copy(s):
        return pltpu.make_async_remote_copy(
            src_ref=near_out.at[s], dst_ref=near_in.at[s],
            send_sem=near_send.at[s], recv_sem=near_recv.at[s],
            device_id={"blk": near_id}, device_id_type=pl.DeviceIdType.MESH,
        )

    def mat_copy(which):
        return pltpu.make_async_remote_copy(
            src_ref=mat_out.at[which, part], dst_ref=mat_in.at[which, part],
            send_sem=mat_send.at[which], recv_sem=mat_recv.at[which],
            device_id={"blk": far_id}, device_id_type=pl.DeviceIdType.MESH,
        )

    def mix_copy():
        return pltpu.make_async_remote_copy(
            src_ref=mix_out, dst_ref=mix_in, send_sem=mix_send, recv_sem=mix_recv,
            device_id={"blk": far_id}, device_id_type=pl.DeviceIdType.MESH,
        )

    def pass_copy(which):
        return pltpu.make_async_remote_copy(
            src_ref=mat_in.at[which, part], dst_ref=mat_in.at[which, part],
            send_sem=pass_send.at[which], recv_sem=pass_recv.at[which],
            device_id={"narrow": mine + 1 - 2 * lax.rem(mine, 2)}, device_id_type=pl.DeviceIdType.MESH,
        )

    def if_far(act):
        pl.when(has_far)(act)

    def send_far(f, value):
        far_out[f] = value
        if_far(lambda: far_copy(f).start())

    def send_near(s, value):
        near_out[s] = value
        near_copy(s).start()

    def from_far(f):
        if_far(lambda: far_copy(f).wait_recv())
        return far_in[f]

    def from_near(s):
        near_copy(s).wait_recv()
        return near_in[s]

    filler = jnp.zeros((LANES - size, 2 * LANES), bf16)

    def field(value):
        return jnp.concatenate([beside(value[:size]), filler, beside(value[size:]), filler], axis=0)

    def solved(which, c, value):
        return product(inverse[which, c], beside(value))

    def put(matrix, which, row, k, block):
        rows = matrix.shape[1] // 2
        high, low = split(block)
        lanes = slice(k * LANES, (k + 1) * LANES)
        matrix[which, row * size:(row + 1) * size, lanes] = high
        matrix[which, rows + row * size:rows + (row + 1) * size, lanes] = low

    nothing = jnp.zeros((size, LANES), f32)

    def place(which, row, blocks):
        def at(c):
            return blocks[c - row] if c - row in blocks else nothing

        for k in range(2):
            put(by_x, which, row, k, at(k))
            put(by_n, which, row, k, at(2 + k))
            if row < 2:
                put(by_y, which, row, k, at(-1 - k))
            else:
                put(by_m, which, row - 2, k, at(5 - k))

    def build_band(c):
        row = row_of(c)
        for k, offset in enumerate(OFFSETS):
            total_a = jnp.zeros((size, size), f32)
            total_e = jnp.zeros((size, size), f32)
            for s in range(3):
                weight = jnp.where(col_ref[row, s] == me * 4 + row + sign * offset, f32(1.0), f32(0.0))
                total_a = total_a + weight * a_off_ref[row, s]
                total_e = total_e + weight * e_off_ref[row, s]
            band[0, c, :, k * LANES:k * LANES + size] = total_a
            band[1, c, :, k * LANES:k * LANES + size] = total_e

    def pack(block):
        rest = block[3 * quarter:, :size]
        third = size // 3
        return jnp.concatenate([
            jnp.concatenate(
                [block[g * quarter:(g + 1) * quarter, :size], rest[:, g * third:(g + 1) * third]], axis=1
            )
            for g in range(3)
        ], axis=0)

    def unpack(packed):
        groups = [packed[g * quarter:(g + 1) * quarter] for g in range(3)]
        whole = jnp.concatenate(
            [group[:, :size] for group in groups]
            + [jnp.concatenate([group[:, size:] for group in groups], axis=1)],
            axis=0,
        )
        return jnp.concatenate([whole, jnp.zeros((size, LANES - size), f32)], axis=1)

    def spans(j):
        first, stop, share = 3 * quarter * j, 3 * quarter * (j + 1), mat_out.shape[2]
        while first < stop:
            piece = first // share
            end = min(stop, (piece + 1) * share)
            yield piece, first - piece * share, end - piece * share
            first = end

    def build_sweep(which, rows, send=True):
        q = shift_ref[which]
        for c in rows:
            merged = product(inverse[which, c], beside(band[0, c] - q * band[1, c]))
            blocks = {o: merged[:, k * LANES:(k + 1) * LANES] for k, o in enumerate(OFFSETS)}
            for j, offset in {0: ((0, -1), (1, -2), (3, 1)), 1: ((2, -2), (4, -1))}.get(c, ()):
                packed, at = pack(blocks[offset]), 0
                for piece, first, stop in spans(j):
                    mat_out[which, piece, first:stop] = packed[at:at + stop - first]
                    at += stop - first
            if c == 1 and send:
                send_mat(which)
            place(which, c, blocks)

    def send_mat(which):
        if_far(lambda: mat_copy(which).start())

    def pass_mat(which):
        @pl.when(has_far)
        def _():
            mat_copy(which).wait_recv()
            if pieces == 2:
                pass_copy(which).start()

    def build_far(which):
        if pieces == 2:
            if_far(lambda: pass_copy(which).wait_recv())
        blocks = [
            unpack(jnp.concatenate([mat_in[which, p, first:stop] for p, first, stop in spans(j)], axis=0))
            for j in range(5)
        ]
        for matrix, rows in (
            (far_x, ((blocks[0], blocks[1]), (blocks[2], nothing))),
            (far_y, ((nothing, blocks[3]), (blocks[4], nothing))),
        ):
            for row, columns in enumerate(rows):
                for k, block in enumerate(columns):
                    put(matrix, which, row, k, block)

    def build_mass():
        for c in range(4):
            blocks = {o: band[1, c, :, k * LANES:(k + 1) * LANES] for k, o in enumerate(OFFSETS)}
            blocks[0] = jnp.concatenate([e_diag_ref[row_of(c)], jnp.zeros((size, LANES - size), f32)], axis=1)
            place(MASS, c, blocks)

    def level(which, k, last=False, late=None, skip=False, aside=None):
        f = which * LEVELS + k
        if aside is not None:
            aside()
        fx = field(state_x[...])
        gx = product(by_x[which], fx)
        n = (state_n[...] - gx[pair:]) - product(by_m[which], field(from_near(f)))
        send_near(f + 1, n)
        fn = field(n)
        if not last:
            gn = product(by_n[which], fn)
            free = base[0] - gn[:pair]
            if not (skip or (which == 0 and late)):
                send_far(f + 2, free)
            state_n[...] = base[1] - gn[pair:]
        if late is not None:
            late()
            if which == 0:
                send_far(f + 2, free)
        if skip:
            y = from_far(f)
        else:
            y = from_far(f) - known[...]
        if skip:
            send_far(f + 2, free)
        fy = field(y)
        x = (state_z[...] - gx[:pair]) - product(by_y[which], fy)
        if not skip:
            known[...] = product(far_y[which], fy) + product(far_x[which], fx)
        if not last:
            state_x[...] = x
            state_z[...] = free
            return None
        fx_last = field(x)
        gx = product(by_x[MASS], fx_last)
        gn = product(by_n[MASS], fn)
        at_n = (gx[pair:] + gn[pair:]) + product(by_m[MASS], field(from_near(f + 1)))

        def at_x():
            y = from_far(f + 1) - known[...]
            return (gx[:pair] + gn[:pair]) + product(by_y[MASS], field(y))

        return at_n, gx[:pair] + gn[:pair], fx_last, at_x

    def begin_field(which):
        gn = product(by_n[which], field(base[1]))
        free = base[0] - gn[:pair]
        send_far(which * LEVELS + 1, free)
        state_x[...] = base[0]
        state_z[...] = free
        state_n[...] = base[1] - gn[pair:]

    def start_with(which, half, values):
        for k, value in enumerate(values):
            base[half, k * size:(k + 1) * size] = solved(which, 2 * half + k, value)

    for load in loads[2:]:
        load.start()
    loads[0].wait()
    loads[1].wait()
    for c in range(4):
        inverse[0, c] = below(inv_ref[0, row_of(c)])
    for half in range(2):
        start_with(0, half, [rhs_ref[rows_of(2 * half + k), :] for k in range(2)])
    pl.semaphore_wait(barrier, greeted)
    send_far(0, base[0])
    send_near(0, base[1])
    tell(0)
    band[...] = jnp.zeros_like(band)
    for load in loads[2:]:
        load.wait()
    for half in range(2):
        for c in (2 * half, 2 * half + 1):
            build_band(c)
        build_sweep(0, (2 * half, 2 * half + 1))

    def post(which):
        def act(b, n):
            pltpu.make_async_remote_copy(
                src_ref=outbox.at[which, b * others + n],
                dst_ref=inbox.at[which, rank],
                send_sem=cross_send.at[which],
                recv_sem=cross_recv.at[which],
                device_id={"blk": b, "narrow": n},
                device_id_type=pl.DeviceIdType.MESH,
            ).start()

        everyone(act)

    def build_mix():
        weights = [
            below(jnp.where(
                parity == 0, zo_ref[:, c * size:(c + 1) * size], zo_ref[:, (3 - c) * size:(4 - c) * size]
            ))
            for c in range(2)
        ]
        blocks = [[band[1, c, :, k * LANES:(k + 1) * LANES] for k in (1, 0)] for c in range(2)]
        mix_out[0] = product(weights[0], beside(blocks[0][0])) + product(weights[1], beside(blocks[1][1]))
        mix_out[1] = product(weights[0], beside(blocks[0][1]))

    def late(which):
        if which == 0:
            build_mix()
            pass_mat(which)
            if_far(lambda: mix_copy().start())
        else:
            hear(2)
        build_far(which)
        f = which * LEVELS
        known[...] = product(far_y[which], field(far_in[f])) + product(far_x[which], field(far_out[f]))

    def mass_aside():
        for c in range(4):
            inverse[1, c] = below(inv_ref[1, row_of(c)])
        build_mass()

    def sweep_aside():
        hear(0)
        build_sweep(1, range(4), send=False)
        zot[...] = below(zo_ref[...])

    def mat_aside():
        send_mat(1)
        hear(1)

    def post_aside():
        for t in range(3, HOOKS):
            hear(t)
        post(0)

    def deal(which):
        def at(d, carry):
            outbox[which, d] = partial[pl.ds(d * per, per), :]
            return carry

        lax.fori_loop(0, devices, at, 0, unroll=8)

    for which in range(2):
        if which == 0:
            begin_field(0)
        level(which, 0, skip=True)
        level(which, 1, late=functools.partial(late, which))
        if which == 0:
            level(which, 2, aside=mass_aside)
            level(which, 3, aside=sweep_aside)
        then = 2 if which else 4

        def step(k, carry):
            level(which, k)
            return carry

        lax.fori_loop(then, SWEEPS - 1, step, 0)
        at_n, ahead, fx, at_x = level(which, SWEEPS - 1, last=True, aside=post_aside if which else mat_aside)

        q = shift_ref[which]
        root = jnp.sqrt(jnp.full((1, LANES), 2.0 * q, f32))
        if which == 1:
            if_far(lambda: mix_copy().wait_recv())
            for half, value in ((1, at_n), (0, ahead)):
                for k in range(2):
                    image[rows_of(2 * half + k), :] = root * value[k * size:(k + 1) * size]
            mixed = below(jnp.concatenate([mix_in[0], mix_in[1]], axis=1))
            partial[...] = product(zot[...], beside(image[...])) + root * product(mixed, fx)
            deal(1)
            post(1)
            inbox[1, rank] = outbox[1, rank]

        for half in (1, 0):
            value = at_n if half else at_x()
            after = []
            for k in range(2):
                mass = value[k * size:(k + 1) * size]
                rows = rows_of(2 * half + k)
                before = rhs_ref[rows, :] if which == 0 else res_ref[rows, :]
                after.append(before + (2.0 * q) * mass)
                res_ref[rows, :] = after[k]
                if which == 0:
                    image[rows, :] = root * mass
            if which == 0:
                start_with(1, half, after)
                if half == 1:
                    send_near(LEVELS, base[1])
                else:
                    send_far(LEVELS, base[0])
        if which == 0:
            begin_field(1)
            partial[...] = product(zot[...], beside(image[...]))
            deal(0)
            pass_mat(1)
            inbox[0, rank] = outbox[0, rank]

    @pl.when(has_far)
    def _():
        def settle(f, carry):
            far_copy(f).wait_send()
            return carry
        lax.fori_loop(0, 2 * LEVELS, settle, 0)
        mix_copy().wait_send()
        for which in range(2):
            mat_copy(which).wait_send()
            if pieces == 2:
                pass_copy(which).wait_send()

    def settle_near(s, carry):
        near_copy(s).wait_send()
        return carry

    lax.fori_loop(0, 2 * LEVELS, settle_near, 0)

    for which in range(2):
        most = pl.ds(0, devices - 1)
        pltpu.make_async_copy(outbox.at[which, most], inbox.at[which, most], cross_recv.at[which]).wait()
        for n in range(others):
            total = inbox[which, n]
            for b in range(1, count):
                total = total + inbox[which, b * others + n]
            cross_ref[:, which, n * LANES:(n + 1) * LANES] = total
        pltpu.make_async_copy(outbox.at[which, most], inbox.at[which, most], cross_send.at[which]).wait()


def shards(count, others, rhs, zo, e_diag, a_off, e_off, col_index, inv_diag, shifts):
    row_count, col_width = rhs.shape
    size = e_diag.shape[1]
    ko = zo.shape[1]
    devices = count * others
    per = ko // devices
    assert row_count == 4 * size and col_width == LANES and count % 2 == 0
    vmem = pl.BlockSpec(memory_space=pltpu.VMEM)
    smem = pl.BlockSpec(memory_space=pltpu.SMEM)
    hbm = pl.BlockSpec(memory_space=pl.ANY)
    pair = 2 * size
    width = 2 * LANES
    pieces = 2 - others % 2
    share = -(-5 * 3 * (size // 4) // (8 * pieces)) * 8
    return pl.pallas_call(
        functools.partial(kernel, count, others, size),
        out_shape=(
            pltpu.VMEM((row_count, col_width), f32),
            pltpu.VMEM((per, 2, others * LANES), f32),
        ),
        in_specs=[hbm, hbm, hbm, hbm, hbm, smem, hbm, smem],
        out_specs=(vmem, vmem),
        scratch_shapes=[
            pltpu.VMEM((2 * LEVELS, pair, LANES), f32),
            pltpu.VMEM((2 * LEVELS, pair, LANES), f32),
            pltpu.VMEM((2 * LEVELS, pair, LANES), f32),
            pltpu.VMEM((2 * LEVELS, pair, LANES), f32),
            pltpu.VMEM((2, pieces, share, LANES), f32),
            pltpu.VMEM((2, pieces, share, LANES), f32),
            pltpu.VMEM((2, ko, LANES), f32),
            pltpu.VMEM((2, ko, LANES), f32),
            *(pltpu.VMEM((pair, LANES), f32) for _ in range(4)),
            pltpu.VMEM((2, pair, LANES), f32),
            pltpu.VMEM((row_count, LANES), f32),
            pltpu.VMEM((2, 4, size, 4 * LANES), f32),
            pltpu.VMEM((3, 4 * pair, width), bf16),
            pltpu.VMEM((3, 4 * pair, width), bf16),
            pltpu.VMEM((3, 2 * pair, width), bf16),
            pltpu.VMEM((3, 2 * pair, width), bf16),
            pltpu.VMEM((2, 2 * pair, width), bf16),
            pltpu.VMEM((2, 2 * pair, width), bf16),
            pltpu.VMEM((2, 4, 2 * size, size), bf16),
            pltpu.VMEM((2 * ko, row_count), bf16),
            pltpu.VMEM((ko, LANES), f32),
            pltpu.VMEM((2, devices, per, LANES), f32),
            pltpu.VMEM((2, devices, per, LANES), f32),
            pltpu.SemaphoreType.DMA((2 * LEVELS,)),
            pltpu.SemaphoreType.DMA((2 * LEVELS,)),
            pltpu.SemaphoreType.DMA((2 * LEVELS,)),
            pltpu.SemaphoreType.DMA((2 * LEVELS,)),
            pltpu.SemaphoreType.DMA((2,)),
            pltpu.SemaphoreType.DMA((2,)),
            pltpu.SemaphoreType.DMA((2,)),
            pltpu.SemaphoreType.DMA((2,)),
            pltpu.SemaphoreType.DMA((2,)),
            pltpu.SemaphoreType.DMA((2,)),
            pltpu.SemaphoreType.DMA,
            pltpu.SemaphoreType.DMA,
            pltpu.SemaphoreType.REGULAR((HOOKS, 2)),
            *(pltpu.VMEM(x.shape, f32) for x in (rhs, zo.T, e_diag, a_off, e_off, inv_diag)),
            pltpu.SemaphoreType.DMA((6,)),
        ],
        compiler_params=pltpu.CompilerParams(
            collective_id=0, has_side_effects=True
        ),
    )(rhs, zo.T, e_diag, a_off, e_off, col_index, inv_diag, shifts)


def solution(mesh):
    placed = (
        P("blk", "narrow"),
        P("blk", None),
        P("blk", None, None),
        P("blk", None, None, None),
        P("blk", None, None, None),
        P("blk", None),
        P(None, "blk", None, None),
        P(),
    )
    return jax.shard_map(
        functools.partial(shards, mesh.shape["blk"], mesh.shape["narrow"]),
        mesh=mesh,
        in_specs=placed,
        out_specs=(P("blk", "narrow"), P(("blk", "narrow"), None, None)),
        check_vma=False,
    )
```
